32 devices in a mesh: dp: 2 (over x), fsdp: 16 (over z, y, core).
Axes of the slice: x: 2, y: 2, z: 4, core: 2. Of those that a mesh axis runs over, the one named last changes fastest.
Arguments:
- tokens: bfloat16 [32768, 1024], P(('dp', 'fsdp')), may hold values from -6 to 6
- time_embed: bfloat16 [32768, 256], P(('dp', 'fsdp')), may hold values from -6 to 6
- segments: int32 [32, 1024], P(('dp', 'fsdp')), may hold values from 0 to 3, never falling along the last dimension, each value on 1 to 512 neighbouring positions
- cotangent: bfloat16 [32768, 1024], P(('dp', 'fsdp')), may hold values from -6 to 6
- attn_norm_gain: bfloat16 [1024], P('fsdp'), may hold values from 0.5 to 1.5
- attn_norm_bias: bfloat16 [1024], P('fsdp'), may hold values from -0.5 to 0.5
- time_weight: bfloat16 [256, 2048], P('fsdp'), may hold values from -0.1875 to 0.1875
- qkv_weight: bfloat16 [1024, 3072], P('fsdp'), may hold values from -0.1875 to 0.1875
- qkv_bias: bfloat16 [3072], P('fsdp'), may hold values from -0.5 to 0.5
- out_weight: bfloat16 [1024, 1024], P('fsdp'), may hold values from -1.5 to 1.5
- out_bias: bfloat16 [1024], P('fsdp'), may hold values from -0.5 to 0.5
- mlp_norm_gain: bfloat16 [1024], P('fsdp'), may hold values from 0.5 to 1.5
- mlp_norm_bias: bfloat16 [1024], P('fsdp'), may hold values from -0.5 to 0.5
- up_weight: bfloat16 [1024, 4096], P('fsdp'), may hold values from -0.1875 to 0.1875
- up_bias: bfloat16 [4096], P('fsdp'), may hold values from -0.5 to 0.5
- down_weight: bfloat16 [4096, 1024], P('fsdp'), may hold values from -0.09375 to 0.09375
- down_bias: bfloat16 [1024], P('fsdp'), may hold values from -0.5 to 0.5
Outputs:
- layer_out: bfloat16 [32768, 1024], P(('dp', 'fsdp'))
- tokens_grad: bfloat16 [32768, 1024], P(('dp', 'fsdp'))
- attn_norm_gain_grad: float32 [1024], P('fsdp')
- attn_norm_bias_grad: float32 [1024], P('fsdp')
- time_weight_grad: float32 [256, 2048], P('fsdp')
- qkv_weight_grad: float32 [1024, 3072], P('fsdp')
- qkv_bias_grad: float32 [3072], P('fsdp')
- out_weight_grad: float32 [1024, 1024], P('fsdp')
- out_bias_grad: float32 [1024], P('fsdp')
- mlp_norm_gain_grad: float32 [1024], P('fsdp')
- mlp_norm_bias_grad: float32 [1024], P('fsdp')
- up_weight_grad: float32 [1024, 4096], P('fsdp')
- up_bias_grad: float32 [4096], P('fsdp')
- down_weight_grad: float32 [4096, 1024], P('fsdp')
- down_bias_grad: float32 [1024], P('fsdp')
The draws below stay inside these ranges and needn't reach their ends.
Inputs may be any that keep to these rules, and one draw needn't show every extreme that they name: `segments`: within each packed row the segment ids never fall, each document holds 1 to 512 tokens, and one document holds exactly 512.
All inputs are finite; a program needn't handle non-finite values.
Results may differ from the reference program's by a relative error of at most 0.015.
Values may be sent and summed in bfloat16 or wider, within the bound.
No kernel may reach another device: no remote copies, remote signals or barrier semaphores. Data moves between devices by JAX's collectives and lax.ppermute only.
A program may use at most 320 MiB of HBM per device.

```python
import math
import jax
import jax.numpy as jnp
import numpy as np
from jax import lax

D = 1024
HEADS = 16
HEAD_DIM = 64
FF = 4096
TIME = 256
SEQ = 1024
ROWS = 32
TOKENS = 32768


def steps_of(stream_key, shape, pieces, smallest, high):
    loudness, own = 1.0, jax.random.fold_in(stream_key, 6)
    for axis_at, parts in pieces:
        heights = jnp.exp(jax.random.uniform(jax.random.fold_in(own, axis_at), (parts,), jnp.float32, smallest / len(pieces), high / len(pieces)))
        loudness = loudness * jnp.repeat(heights, shape[axis_at] // parts).reshape([-1 if axis == axis_at else 1 for axis in range(len(shape))])
    return loudness


def length_profile(count, total, limit, skew):
    loads = [(1 << 20) // math.isqrt(rank ** skew) + 1 for rank in range(2, count + 1)]
    spare, given = total - limit - (count - 1), [1] * (count - 1)
    while spare > 0:
        movable = [i for i in range(count - 1) if given[i] < limit]
        whole, left = sum([loads[i] for i in movable]), spare
        for i in movable:
            more = min(limit - given[i], max(1, left * loads[i] // whole), spare)
            given[i] = given[i] + more
            spare = spare - more
    return np.array([limit] + given)


def ragged(rng, count, total, reach, slope):
    if count == 2:
        one = jax.random.randint(rng, (), max(1, total - reach), min(reach, total - 1) + 1)
        return jnp.stack([one, total - one])
    tallies = jnp.asarray(length_profile(count, total, reach, slope), jnp.int32)
    couples = (count - 1) // 2
    giver, receiver = tallies[1:1 + 2 * couples:2], tallies[2:2 + 2 * couples:2]
    slack = jnp.minimum(giver - 1, reach - receiver)
    moved = jax.random.randint(jax.random.fold_in(rng, 1), (couples,), 0, 1 << 20) % (slack + 1)
    tallies = tallies.at[1:1 + 2 * couples:2].set(giver - moved).at[2:2 + 2 * couples:2].set(receiver + moved)
    return tallies[jax.random.permutation(jax.random.fold_in(rng, 2), count)]


def normal_values(key, extent, scale, reach, split=(), kind=jnp.bfloat16):
    level = steps_of(key, extent, split, -0.22, 0.18) if split else 1.0
    drawn = jax.random.normal(key, extent, jnp.float32) * scale * level
    return jnp.minimum(jnp.maximum(drawn, -reach), reach).astype(kind)


def setup_inputs(seed: int = 0) -> dict:
    arg_keys = jax.random.split(jax.random.key(seed), 18)
    return {
        "tokens": normal_values(arg_keys[0], (TOKENS, D), 1.0, 6.0, ((0, 32),)),
        "time_embed": normal_values(arg_keys[1], (TOKENS, TIME), 1.0, 6.0, ((0, 32),)),
        "segments": jax.vmap(lambda own: jnp.searchsorted(jnp.cumsum(ragged(own, 4, SEQ, SEQ // 2, 1)), jnp.arange(SEQ), side="right"))(jax.random.split(arg_keys[2], ROWS)).reshape((ROWS, SEQ)).astype(jnp.int32),
        "cotangent": normal_values(arg_keys[3], (TOKENS, D), 1.0, 6.0, ((0, 32),)),
        "attn_norm_gain": jnp.clip(1.0 + 0.1 * jax.random.normal(arg_keys[4], (D,), jnp.float32), 0.5, 1.5).astype(jnp.bfloat16),
        "attn_norm_bias": jnp.clip(jax.random.uniform(arg_keys[5], (D,), jnp.float32, -0.5, 0.5) * steps_of(arg_keys[5], (D,), ((0, 16),), -0.4, 0.0), -0.5, 0.5).astype(jnp.bfloat16),
        "time_weight": normal_values(arg_keys[6], (TIME, 2 * D), (4 * TIME) ** -0.5, 0.1875, ((0, 16),)),
        "qkv_weight": normal_values(arg_keys[7], (D, 3 * D), D ** -0.5, 0.1875, ((0, 16),)),
        "qkv_bias": jnp.clip(jax.random.uniform(arg_keys[8], (3 * D,), jnp.float32, -0.5, 0.5) * steps_of(arg_keys[8], (3 * D,), ((0, 16),), -0.4, 0.0), -0.5, 0.5).astype(jnp.bfloat16),
        "out_weight": normal_values(arg_keys[9], (D, D), (D // 64) ** -0.5, 1.5, ((0, 16),)),
        "out_bias": jnp.clip(jax.random.uniform(arg_keys[10], (D,), jnp.float32, -0.5, 0.5) * steps_of(arg_keys[10], (D,), ((0, 16),), -0.4, 0.0), -0.5, 0.5).astype(jnp.bfloat16),
        "mlp_norm_gain": jnp.clip(1.0 + 0.1 * jax.random.normal(arg_keys[11], (D,), jnp.float32), 0.5, 1.5).astype(jnp.bfloat16),
        "mlp_norm_bias": jnp.clip(jax.random.uniform(arg_keys[12], (D,), jnp.float32, -0.5, 0.5) * steps_of(arg_keys[12], (D,), ((0, 16),), -0.4, 0.0), -0.5, 0.5).astype(jnp.bfloat16),
        "up_weight": normal_values(arg_keys[13], (D, FF), D ** -0.5, 0.1875, ((0, 16),)),
        "up_bias": jnp.clip(jax.random.uniform(arg_keys[14], (FF,), jnp.float32, -0.5, 0.5) * steps_of(arg_keys[14], (FF,), ((0, 16),), -0.4, 0.0), -0.5, 0.5).astype(jnp.bfloat16),
        "down_weight": normal_values(arg_keys[15], (FF, D), FF ** -0.5, 0.09375, ((0, 16),)),
        "down_bias": jnp.clip(jax.random.uniform(arg_keys[16], (D,), jnp.float32, -0.5, 0.5) * steps_of(arg_keys[16], (D,), ((0, 16),), -0.4, 0.0), -0.5, 0.5).astype(jnp.bfloat16),
    }


@jax.custom_vjp
def low(v):
    return lax.optimization_barrier(v.astype(jnp.bfloat16)).astype(jnp.float32)

@jax.custom_vjp
def low_back(v):
    return v

def low_keep(v):
    return (low(v), None)

def low_pass(kept, grad):
    return (grad,)

def back_keep(v):
    return (v, None)

def back_low(kept, grad):
    return (low(grad),)
low.defvjp(low_keep, low_pass)
low_back.defvjp(back_keep, back_low)

def matmul(left, right):
    return jnp.dot(left, right, precision=lax.Precision.HIGHEST)

def positions_of(segments):
    index = jnp.broadcast_to(jnp.arange(segments.shape[1], dtype=jnp.int32), segments.shape)
    starts = jnp.concatenate([jnp.ones((segments.shape[0], 1), dtype=bool), segments[:, 1:] != segments[:, :-1]], axis=1)
    first = lax.cummax(jnp.where(starts, index, jnp.zeros_like(index)), axis=1)
    return index - first

def rotary_tables(positions, head_width):
    steps_half = jnp.arange(head_width // 2, dtype=jnp.float32)
    inverse = jnp.exp(steps_half * (-2.0 * math.log(10000.0) / head_width))
    angles = positions.astype(jnp.float32)[..., None] * inverse
    return (jnp.cos(angles), jnp.sin(angles))

def rotate(values, cosine, sine):
    half = values.shape[-1] // 2
    first, second = (values[..., :half], values[..., half:])
    cosine = cosine[..., None, :]
    sine = sine[..., None, :]
    return jnp.concatenate([first * cosine - second * sine, second * cosine + first * sine], axis=-1)

def norm_mod(values, gain, bias, shift):
    center = lax.optimization_barrier(jnp.mean(values, axis=-1, keepdims=True))
    centered = values - center
    spread = lax.optimization_barrier(jnp.mean(centered * centered, axis=-1, keepdims=True))
    return (centered * lax.rsqrt(spread + 1e-05) * gain + bias) * (1.0 + shift)

def attend_row(item):
    query, key, value, seg = item
    scale = query.shape[-1] ** (-0.5)
    raw = low_back(jnp.einsum('qhd,khd->hqk', query, key, precision=lax.Precision.HIGHEST))
    same = (seg[:, None] == seg[None, :])[None]
    scores = jnp.where(same, raw * scale, -1e+30)
    peak = lax.optimization_barrier(jnp.max(scores, axis=-1, keepdims=True))
    expo = jnp.exp(scores - peak)
    probs = expo / lax.optimization_barrier(jnp.sum(expo, axis=-1, keepdims=True))
    return jnp.einsum('hqk,khd->qhd', low(probs), value, precision=lax.Precision.HIGHEST)

def layer(tokens, time_embed, segments, attn_norm_gain, attn_norm_bias, time_weight, qkv_weight, qkv_bias, out_weight, out_bias, mlp_norm_gain, mlp_norm_bias, up_weight, up_bias, down_weight, down_bias):
    rows, seq = segments.shape
    modulation = low_back(matmul(time_embed, time_weight))
    normed_one = low(norm_mod(tokens, attn_norm_gain, attn_norm_bias, modulation[:, :D]))
    qkv = low_back(matmul(normed_one, qkv_weight)) + qkv_bias
    heads = qkv.reshape(rows, seq, 3, HEADS, HEAD_DIM)
    cosine, sine = rotary_tables(positions_of(segments), HEAD_DIM)
    query = low(rotate(heads[:, :, 0], cosine, sine))
    key = low(rotate(heads[:, :, 1], cosine, sine))
    value = low(heads[:, :, 2])
    mixed = lax.map(jax.checkpoint(attend_row), (query, key, value, segments))
    mixed = low(low_back(mixed.reshape(rows * seq, D)))
    hidden = tokens + low_back(matmul(mixed, out_weight)) + out_bias
    normed_two = low(norm_mod(hidden, mlp_norm_gain, mlp_norm_bias, modulation[:, D:]))
    up = low_back(matmul(normed_two, up_weight)) + up_bias
    active = low(jax.nn.gelu(up, approximate=False))
    return hidden + low_back(matmul(active, down_weight)) + down_bias

def reference(tokens, time_embed, segments, cotangent, attn_norm_gain, attn_norm_bias, time_weight, qkv_weight, qkv_bias, out_weight, out_bias, mlp_norm_gain, mlp_norm_bias, up_weight, up_bias, down_weight, down_bias):
    params = tuple((p.astype(jnp.float32) for p in (attn_norm_gain, attn_norm_bias, time_weight, qkv_weight, qkv_bias, out_weight, out_bias, mlp_norm_gain, mlp_norm_bias, up_weight, up_bias, down_weight, down_bias)))
    time_float = time_embed.astype(jnp.float32)

    def forward(inputs, *weights):
        return layer(inputs, time_float, segments, *weights)
    output, pull = jax.vjp(forward, tokens.astype(jnp.float32), *params)
    grads = pull(cotangent.astype(jnp.float32))
    factor = TOKENS ** (-0.5)
    return (output.astype(jnp.bfloat16), grads[0].astype(jnp.bfloat16), grads[1] * factor, grads[2] * factor, grads[3] * factor, grads[4] * factor, grads[5] * factor, grads[6] * factor, grads[7] * factor, grads[8] * factor, grads[9] * factor, grads[10] * factor, grads[11] * factor, grads[12] * factor, grads[13] * factor)
```

```python
import functools
import math

import jax
import jax.numpy as jnp
from jax import lax
from jax.experimental import pallas as pl
from jax.experimental.pallas import tpu as pltpu
from jax.sharding import PartitionSpec as P

HEADS = 16
HEAD_DIM = 64
LANES = 128
BLOCK = 256


def positions_of(segments):
    index = jnp.broadcast_to(jnp.arange(segments.shape[1], dtype=jnp.int32), segments.shape)
    starts = jnp.concatenate(
        [jnp.ones((segments.shape[0], 1), dtype=bool), segments[:, 1:] != segments[:, :-1]], axis=1
    )
    first = lax.cummax(jnp.where(starts, index, jnp.zeros_like(index)), axis=1)
    return index - first


def rotary_tables(positions, head_width):
    steps_half = jnp.arange(head_width // 2, dtype=jnp.float32)
    inverse = jnp.exp(steps_half * (-2.0 * math.log(10000.0) / head_width))
    angles = positions.astype(jnp.float32)[..., None] * inverse
    return (jnp.cos(angles), jnp.sin(angles))


def block_bounds(segments, block):
    rows, seq = segments.shape
    parts = segments.reshape(rows, seq // block, block)
    first, last = (parts[:, :, 0], parts[:, :, -1])
    low = jnp.sum((last[:, None, :] < first[:, :, None]).astype(jnp.int32), axis=-1)
    high = jnp.sum((first[:, None, :] <= last[:, :, None]).astype(jnp.int32), axis=-1)
    return (low, high - low)


def partner(values, lane):
    ahead = pltpu.roll(values, LANES - HEAD_DIM // 2, 1)
    behind = pltpu.roll(values, HEAD_DIM // 2, 1)
    return jnp.where(lane % HEAD_DIM < HEAD_DIM // 2, ahead, behind)


def head_masks():
    lane = lax.broadcasted_iota(jnp.int32, (1, LANES), 1)
    own = (lane < HEAD_DIM).astype(jnp.float32)
    return (own.astype(jnp.bfloat16), (1.0 - own).astype(jnp.bfloat16))


def dot_nt(left, right):
    return lax.dot_general(
        left, right, (((1,), (1,)), ((), ())), preferred_element_type=jnp.float32
    )


def dot_tn(left, right):
    return lax.dot_general(
        left, right, (((0,), (0,)), ((), ())), preferred_element_type=jnp.float32
    )


def same_document(col_ref, row_ref, start, size, at, block):
    col = col_ref[pl.ds(start, size), :]
    row = row_ref[0, :, pl.ds(at, block)]
    return jnp.concatenate([col] * (block // LANES), axis=1) == row


def forward_kernel(
    low_ref, count_ref, q_ref, k_ref, v_ref, cos_ref, sin_ref, col_ref, row_ref,
    mixed_ref, query_ref, key_ref, value_ref, lse_ref, *, block
):
    row_at = pl.program_id(0)
    seq = q_ref.shape[0]
    blocks = seq // block
    lane = lax.broadcasted_iota(jnp.int32, (seq, LANES), 1)
    cosine, sine = (cos_ref[...], sin_ref[...])
    q, k = (q_ref[...], k_ref[...])
    rotated = q * cosine + partner(q, lane) * sine
    query_ref[...] = rotated.astype(jnp.bfloat16) * jnp.bfloat16(HEAD_DIM**-0.5)
    key_ref[...] = (k * cosine + partner(k, lane) * sine).astype(jnp.bfloat16)
    value_ref[...] = v_ref[...].astype(jnp.bfloat16)
    masks = head_masks()

    def one_block(i, carry):
        at = pl.multiple_of(i * block, block)
        low = low_ref[row_at, i]
        count = count_ref[row_at, i]
        start = pl.multiple_of(low * block, block)
        for size_at in range(1, blocks + 1):

            @pl.when(count == size_at)
            def _(size=size_at * block):
                keys = key_ref[pl.ds(start, size), :]
                values = value_ref[pl.ds(start, size), :]
                query = query_ref[pl.ds(at, block), :]
                same = same_document(col_ref, row_ref, start, size, at, block)
                weights = []
                for head in range(2):
                    scores = jnp.where(same, dot_nt(keys, query * masks[head]), -1e30)
                    peak = jnp.max(scores, axis=0, keepdims=True)
                    expo = jnp.exp(scores - peak)
                    total = jnp.sum(expo, axis=0, keepdims=True)
                    lse_ref[0, pl.ds(head, 1), pl.ds(at, block)] = peak + jnp.log(total)
                    weights.append((expo * (1.0 / total)).astype(jnp.bfloat16))
                mixed = dot_tn(weights[0], values * masks[0]) + dot_tn(
                    weights[1], values * masks[1]
                )
                mixed_ref[pl.ds(at, block), :] = mixed.astype(jnp.bfloat16)

        return carry

    lax.fori_loop(0, blocks, one_block, 0)


def backward_kernel(
    low_ref, count_ref, query_ref, key_ref, value_ref, grad_ref, lse_ref, cos_ref, sin_ref,
    col_ref, row_ref, gq_ref, gk_ref, gv_ref, bias_ref, dq_acc, dk_acc, dv_acc, *, block
):
    row_at = pl.program_id(0)
    seq = query_ref.shape[0]
    blocks = seq // block
    dk_acc[...] = jnp.zeros_like(dk_acc)
    dv_acc[...] = jnp.zeros_like(dv_acc)
    masks = head_masks()

    def one_block(i, carry):
        at = pl.multiple_of(i * block, block)
        low = low_ref[row_at, i]
        count = count_ref[row_at, i]
        start = pl.multiple_of(low * block, block)
        for size_at in range(1, blocks + 1):

            @pl.when(count == size_at)
            def _(size=size_at * block):
                keys = key_ref[pl.ds(start, size), :]
                values = value_ref[pl.ds(start, size), :]
                query = query_ref[pl.ds(at, block), :]
                grad = grad_ref[pl.ds(at, block), :]
                same = same_document(col_ref, row_ref, start, size, at, block)
                dq = jnp.zeros((block, LANES), jnp.float32)
                dk = jnp.zeros((size, LANES), jnp.float32)
                dv = jnp.zeros((size, LANES), jnp.float32)
                for head in range(2):
                    own_query = query * masks[head]
                    own_grad = grad * masks[head]
                    scores = jnp.where(same, dot_nt(keys, own_query), -1e30)
                    lse = lse_ref[0, pl.ds(head, 1), pl.ds(at, block)]
                    probs = jnp.exp(scores - lse)
                    grad_probs = dot_nt(values, own_grad)
                    inner = jnp.sum(probs * grad_probs, axis=0, keepdims=True)
                    grad_raw = (probs * (grad_probs - inner)).astype(jnp.bfloat16)
                    dv = dv + jnp.dot(
                        probs.astype(jnp.bfloat16), own_grad, preferred_element_type=jnp.float32
                    )
                    dk = dk + jnp.dot(grad_raw, own_query, preferred_element_type=jnp.float32)
                    dq = dq + dot_tn(grad_raw, keys * masks[head])
                dq_acc[pl.ds(at, block), :] = dq
                dk_acc[pl.ds(start, size), :] += dk
                dv_acc[pl.ds(start, size), :] += dv

        return carry

    lax.fori_loop(0, blocks, one_block, 0)
    lane = lax.broadcasted_iota(jnp.int32, (seq, LANES), 1)
    cosine, sine = (cos_ref[...], sin_ref[...])
    dq = dq_acc[...] * (HEAD_DIM**-0.5)
    dk = dk_acc[...]
    dv = dv_acc[...]
    gq = dq * cosine - partner(dq, lane) * sine
    gk = dk * cosine - partner(dk, lane) * sine
    gq_ref[...] = gq.astype(jnp.bfloat16)
    gk_ref[...] = gk.astype(jnp.bfloat16)
    gv_ref[...] = dv.astype(jnp.bfloat16)
    bias_ref[0, 0:1, :] = jnp.sum(gq, axis=0, keepdims=True)
    bias_ref[0, 1:2, :] = jnp.sum(gk, axis=0, keepdims=True)
    bias_ref[0, 2:3, :] = jnp.sum(dv, axis=0, keepdims=True)


def attention_tables(segments):
    rows, seq = segments.shape
    cosine, sine = rotary_tables(positions_of(segments), HEAD_DIM)
    reach = (rows * seq, HEAD_DIM // 2)
    cosine, sine = (cosine.reshape(reach), sine.reshape(reach))
    cos_wide = jnp.concatenate([cosine] * 4, axis=1)
    sin_wide = jnp.concatenate([-sine, sine] * 2, axis=1)
    col = jnp.broadcast_to(segments.reshape(rows * seq, 1), (rows * seq, LANES))
    row = segments.reshape(rows, 1, seq)
    return (cos_wide, sin_wide, col, row)


def attend_forward(qkv, tables, bounds, block):
    cos_wide, sin_wide, col, row = tables
    rows, _, seq = row.shape
    width = qkv.shape[1] // 3
    pairs = width // LANES
    tile = lambda shift: pl.BlockSpec((seq, LANES), lambda r, h, *_: (r, h + shift))
    whole = pl.BlockSpec((seq, LANES), lambda r, h, *_: (r, 0))
    lines = pl.BlockSpec((1, 1, seq), lambda r, h, *_: (r, 0, 0))
    low = jax.ShapeDtypeStruct((rows * seq, width), jnp.bfloat16)
    return pl.pallas_call(
        functools.partial(forward_kernel, block=block),
        grid_spec=pltpu.PrefetchScalarGridSpec(
            num_scalar_prefetch=2,
            grid=(rows, pairs),
            in_specs=[tile(0), tile(pairs), tile(2 * pairs), whole, whole, whole, lines],
            out_specs=[
                tile(0), tile(0), tile(0), tile(0),
                pl.BlockSpec((1, 2, seq), lambda r, h, *_: (r * pairs + h, 0, 0)),
            ],
        ),
        out_shape=[low, low, low, low, jax.ShapeDtypeStruct((rows * pairs, 2, seq), jnp.float32)],
        name="attend_forward",
    )(*bounds, qkv, qkv, qkv, cos_wide, sin_wide, col, row)


def attend_backward(query, key, value, grad_mixed, lse, tables, bounds, block):
    cos_wide, sin_wide, col, row = tables
    rows, _, seq = row.shape
    width = query.shape[1]
    pairs = width // LANES
    tile = pl.BlockSpec((seq, LANES), lambda r, h, *_: (r, h))
    whole = pl.BlockSpec((seq, LANES), lambda r, h, *_: (r, 0))
    lines = pl.BlockSpec((1, 1, seq), lambda r, h, *_: (r, 0, 0))
    low = jax.ShapeDtypeStruct((rows * seq, width), jnp.bfloat16)
    acc = pltpu.VMEM((seq, LANES), jnp.float32)
    return pl.pallas_call(
        functools.partial(backward_kernel, block=block),
        grid_spec=pltpu.PrefetchScalarGridSpec(
            num_scalar_prefetch=2,
            grid=(rows, pairs),
            in_specs=[
                tile, tile, tile, tile,
                pl.BlockSpec((1, 2, seq), lambda r, h, *_: (r * pairs + h, 0, 0)),
                whole, whole, whole, lines,
            ],
            out_specs=[
                tile, tile, tile,
                pl.BlockSpec((1, 3, LANES), lambda r, h, *_: (r, 0, h)),
            ],
            scratch_shapes=[acc, acc, acc],
        ),
        out_shape=[low, low, low, jax.ShapeDtypeStruct((rows, 3, width), jnp.float32)],
        name="attend_backward",
    )(*bounds, query, key, value, grad_mixed, lse, cos_wide, sin_wide, col, row)


def norm_mod(values, gain, bias, shift):
    center = jnp.mean(values, axis=-1, keepdims=True)
    centered = values - center
    spread = jnp.mean(centered * centered, axis=-1, keepdims=True)
    return (centered * lax.rsqrt(spread + 1e-05) * gain + bias) * (1.0 + shift)


def gelu_exact(values):
    return jax.nn.gelu(values, approximate=False)


def product(left, right):
    return jnp.dot(left, right, preferred_element_type=jnp.float32)


def product_left(left, right):
    return lax.dot_general(
        left, right, (((0,), (0,)), ((), ())), preferred_element_type=jnp.float32
    )


def product_right(left, right):
    return lax.dot_general(
        left, right, (((1,), (1,)), ((), ())), preferred_element_type=jnp.float32
    )


def gather(part):
    return lax.all_gather(part, "fsdp", axis=0, tiled=True)


def pack(parts, rows):
    flat = jnp.concatenate(parts, axis=-1)
    room = rows * LANES * -(-flat.shape[-1] // (rows * LANES))
    flat = jnp.pad(flat, ((0, 0), (0, room - flat.shape[-1])))
    return flat.reshape(flat.shape[0] * rows, room // rows)


def unpack(packed, sizes, shards):
    flat = packed.reshape(shards, -1)
    parts, at = ([], 0)
    for size in sizes:
        parts.append(flat[:, at : at + size].reshape(-1))
        at += size
    return parts


def reduce_weight(partial):
    share = lax.psum_scatter(
        partial.astype(jnp.bfloat16), "fsdp", scatter_dimension=0, tiled=True
    )
    if lax.axis_size("dp") == 2:
        other = lax.ppermute(share, "dp", [(0, 1), (1, 0)])
        return share.astype(jnp.float32) + other.astype(jnp.float32)
    return lax.psum(share.astype(jnp.float32), "dp")


def per_device(
    tokens,
    time_embed,
    segments,
    cotangent,
    attn_norm_gain,
    attn_norm_bias,
    time_weight,
    qkv_weight,
    qkv_bias,
    out_weight,
    out_bias,
    mlp_norm_gain,
    mlp_norm_bias,
    up_weight,
    up_bias,
    down_weight,
    down_bias,
):
    width = tokens.shape[1]
    rows, seq = segments.shape
    shards = lax.axis_size("fsdp")
    total_tokens = tokens.shape[0] * lax.axis_size("dp") * shards
    factor = 1.0 / math.sqrt(total_tokens)
    block = min(BLOCK, seq)
    time_rows, time_cols = time_weight.shape

    small = (
        attn_norm_gain, attn_norm_bias, qkv_bias, out_bias,
        mlp_norm_gain, mlp_norm_bias, up_bias, down_bias,
    )
    sizes = [part.shape[0] for part in small]
    first = jnp.concatenate([time_weight, pack([p[None] for p in small], time_rows)], axis=1)
    first = gather(first)
    w_qkv = gather(qkv_weight)
    w_out = gather(out_weight)
    w_up = gather(up_weight)
    w_down = gather(down_weight)
    w_time = first[:, :time_cols]
    gain_one, bias_one, b_qkv, b_out, gain_two, bias_two, b_up, b_down = (
        part.astype(jnp.float32) for part in unpack(first[:, time_cols:], sizes, shards)
    )

    tables = attention_tables(segments)
    bounds = block_bounds(segments, block)
    modulation = product(time_embed, w_time)
    tokens_float = tokens.astype(jnp.float32)
    norm_one, pull_one = jax.vjp(
        norm_mod, tokens_float, gain_one, bias_one, modulation[:, :width]
    )
    normed_one = norm_one.astype(jnp.bfloat16)
    qkv = product(normed_one, w_qkv) + b_qkv
    mixed, query, key, value, lse = attend_forward(qkv, tables, bounds, block)
    hidden = tokens_float + product(mixed, w_out) + b_out
    norm_two, pull_two = jax.vjp(norm_mod, hidden, gain_two, bias_two, modulation[:, width:])
    normed_two = norm_two.astype(jnp.bfloat16)
    up = product(normed_two, w_up) + b_up
    active_float, pull_gelu = jax.vjp(gelu_exact, up)
    active = active_float.astype(jnp.bfloat16)
    grad_out = cotangent.astype(jnp.float32)
    down_share = reduce_weight(product_left(active, cotangent))
    output = hidden + product(active, w_down) + b_down
    layer_out = output.astype(jnp.bfloat16)

    down_bias_sum = jnp.sum(grad_out, axis=0)
    grad_active = product_right(cotangent, w_down)
    (grad_up,) = pull_gelu(grad_active)
    up_bias_sum = jnp.sum(grad_up, axis=0)
    grad_up_low = grad_up.astype(jnp.bfloat16)
    up_share = reduce_weight(product_left(normed_two, grad_up_low))
    grad_normed_two = product_right(grad_up_low, w_up)
    grad_hidden_part, gain_two_sum, bias_two_sum, grad_shift_two = pull_two(grad_normed_two)
    grad_hidden = grad_out + grad_hidden_part
    out_bias_sum = jnp.sum(grad_hidden, axis=0)
    grad_hidden_low = grad_hidden.astype(jnp.bfloat16)
    out_share = reduce_weight(product_left(mixed, grad_hidden_low))
    grad_mixed = product_right(grad_hidden_low, w_out).astype(jnp.bfloat16)
    grad_query, grad_key, grad_value, qkv_bias_rows = attend_backward(
        query, key, value, grad_mixed, lse, tables, bounds, block
    )
    qkv_bias_sum = jnp.sum(qkv_bias_rows, axis=0).reshape(-1)
    grad_qkv_low = jnp.concatenate([grad_query, grad_key, grad_value], axis=1)
    qkv_share = reduce_weight(product_left(normed_one, grad_qkv_low))
    grad_normed_one = product_right(grad_qkv_low, w_qkv)
    grad_tokens_part, gain_one_sum, bias_one_sum, grad_shift_one = pull_one(grad_normed_one)
    tokens_grad = (grad_hidden + grad_tokens_part).astype(jnp.bfloat16)
    grad_shift = jnp.concatenate([grad_shift_one, grad_shift_two], axis=1).astype(jnp.bfloat16)
    time_sum = product_left(time_embed, grad_shift)
    small_sums = (
        gain_one_sum, bias_one_sum, qkv_bias_sum, out_bias_sum,
        gain_two_sum, bias_two_sum, up_bias_sum, down_bias_sum,
    )
    packed = pack([part.reshape(shards, -1) for part in small_sums], time_rows)
    last_share = reduce_weight(jnp.concatenate([time_sum, packed], axis=1))
    smalls = unpack(last_share[:, time_cols:] * factor, sizes, 1)
    return (
        layer_out,
        tokens_grad,
        smalls[0],
        smalls[1],
        last_share[:, :time_cols] * factor,
        qkv_share * factor,
        smalls[2],
        out_share * factor,
        smalls[3],
        smalls[4],
        smalls[5],
        up_share * factor,
        smalls[6],
        down_share * factor,
        smalls[7],
    )


def solution(mesh):
    placed = (
        P(("dp", "fsdp"), None),
        P(("dp", "fsdp"), None),
        P(("dp", "fsdp"), None),
        P(("dp", "fsdp"), None),
        P("fsdp"),
        P("fsdp"),
        P("fsdp", None),
        P("fsdp", None),
        P("fsdp"),
        P("fsdp", None),
        P("fsdp"),
        P("fsdp"),
        P("fsdp"),
        P("fsdp", None),
        P("fsdp"),
        P("fsdp", None),
        P("fsdp"),
    )
    return jax.shard_map(
        per_device,
        mesh=mesh,
        in_specs=placed,
        out_specs=(
            P(("dp", "fsdp"), None),
            P(("dp", "fsdp"), None),
            P("fsdp"),
            P("fsdp"),
            P("fsdp", None),
            P("fsdp", None),
            P("fsdp"),
            P("fsdp", None),
            P("fsdp"),
            P("fsdp"),
            P("fsdp"),
            P("fsdp", None),
            P("fsdp"),
            P("fsdp", None),
            P("fsdp"),
        ),
        check_vma=False,
    )
```

```python
import functools
import math

import jax
import jax.numpy as jnp
from jax import lax
from jax.experimental import pallas as pl
from jax.experimental.pallas import tpu as pltpu
from jax.sharding import PartitionSpec as P


HEAD_DIM = 64
LANES = 128
BLOCK = 256


def positions_of(segments):
    index = jnp.broadcast_to(jnp.arange(segments.shape[1], dtype=jnp.int32), segments.shape)
    starts = jnp.concatenate(
        [jnp.ones((segments.shape[0], 1), dtype=bool), segments[:, 1:] != segments[:, :-1]], axis=1
    )
    first = lax.cummax(jnp.where(starts, index, jnp.zeros_like(index)), axis=1)
    return index - first


def rotary_tables(positions, head_width):
    steps_half = jnp.arange(head_width // 2, dtype=jnp.float32)
    inverse = jnp.exp(steps_half * (-2.0 * math.log(10000.0) / head_width))
    angles = positions.astype(jnp.float32)[..., None] * inverse
    return (jnp.cos(angles), jnp.sin(angles))


def block_bounds(segments, block):
    rows, seq = segments.shape
    parts = segments.reshape(rows, seq // block, block)
    first, last = (parts[:, :, 0], parts[:, :, -1])
    low = jnp.sum((last[:, None, :] < first[:, :, None]).astype(jnp.int32), axis=-1)
    high = jnp.sum((first[:, None, :] <= last[:, :, None]).astype(jnp.int32), axis=-1)
    return (low, high - low)


def partner(values, lane):
    ahead = pltpu.roll(values, LANES - HEAD_DIM // 2, 1)
    behind = pltpu.roll(values, HEAD_DIM // 2, 1)
    return jnp.where(lane % HEAD_DIM < HEAD_DIM // 2, ahead, behind)


def head_masks():
    lane = lax.broadcasted_iota(jnp.int32, (1, LANES), 1)
    own = (lane < HEAD_DIM).astype(jnp.float32)
    return (own.astype(jnp.bfloat16), (1.0 - own).astype(jnp.bfloat16))


def dot_nt(left, right):
    return lax.dot_general(
        left, right, (((1,), (1,)), ((), ())), preferred_element_type=jnp.float32
    )


def dot_tn(left, right):
    return lax.dot_general(
        left, right, (((0,), (0,)), ((), ())), preferred_element_type=jnp.float32
    )


def same_document(col_ref, row_ref, start, size, at, block):
    col = col_ref[pl.ds(start, size), :]
    row = row_ref[0, :, pl.ds(at, block)]
    return jnp.concatenate([col] * (block // LANES), axis=1) == row


def forward_kernel(
    low_ref, count_ref, q_ref, k_ref, v_ref, cos_ref, sin_ref, col_ref, row_ref,
    mixed_ref, query_ref, key_ref, value_ref, lse_ref, *, block
):
    row_at = pl.program_id(0)
    seq = q_ref.shape[0]
    blocks = seq // block
    lane = lax.broadcasted_iota(jnp.int32, (seq, LANES), 1)
    cosine, sine = (cos_ref[...], sin_ref[...])
    q, k = (q_ref[...], k_ref[...])
    rotated = q * cosine + partner(q, lane) * sine
    query_ref[...] = rotated.astype(jnp.bfloat16) * jnp.bfloat16(HEAD_DIM**-0.5)
    key_ref[...] = (k * cosine + partner(k, lane) * sine).astype(jnp.bfloat16)
    value_ref[...] = v_ref[...].astype(jnp.bfloat16)
    masks = head_masks()

    def one_block(i, carry):
        at = pl.multiple_of(i * block, block)
        low = low_ref[row_at, i]
        count = count_ref[row_at, i]
        start = pl.multiple_of(low * block, block)
        for size_at in range(1, blocks + 1):

            @pl.when(count == size_at)
            def _(size=size_at * block):
                keys = key_ref[pl.ds(start, size), :]
                values = value_ref[pl.ds(start, size), :]
                query = query_ref[pl.ds(at, block), :]
                same = same_document(col_ref, row_ref, start, size, at, block)
                weights = []
                for head in range(2):
                    scores = jnp.where(same, dot_nt(keys, query * masks[head]), -1e30)
                    peak = jnp.max(scores, axis=0, keepdims=True)
                    expo = jnp.exp(scores - peak)
                    total = jnp.sum(expo, axis=0, keepdims=True)
                    lse_ref[0, pl.ds(head, 1), pl.ds(at, block)] = peak + jnp.log(total)
                    weights.append((expo * (1.0 / total)).astype(jnp.bfloat16))
                mixed = dot_tn(weights[0], values * masks[0]) + dot_tn(
                    weights[1], values * masks[1]
                )
                mixed_ref[pl.ds(at, block), :] = mixed.astype(jnp.bfloat16)

        return carry

    lax.fori_loop(0, blocks, one_block, 0)


def backward_kernel(
    low_ref, count_ref, query_ref, key_ref, value_ref, grad_ref, lse_ref, cos_ref, sin_ref,
    col_ref, row_ref, gq_ref, gk_ref, gv_ref, bias_ref, dq_acc, dk_acc, dv_acc, *, block
):
    row_at = pl.program_id(0)
    seq = query_ref.shape[0]
    blocks = seq // block
    dk_acc[...] = jnp.zeros_like(dk_acc)
    dv_acc[...] = jnp.zeros_like(dv_acc)
    masks = head_masks()

    def one_block(i, carry):
        at = pl.multiple_of(i * block, block)
        low = low_ref[row_at, i]
        count = count_ref[row_at, i]
        start = pl.multiple_of(low * block, block)
        for size_at in range(1, blocks + 1):

            @pl.when(count == size_at)
            def _(size=size_at * block):
                keys = key_ref[pl.ds(start, size), :]
                values = value_ref[pl.ds(start, size), :]
                query = query_ref[pl.ds(at, block), :]
                grad = grad_ref[pl.ds(at, block), :]
                same = same_document(col_ref, row_ref, start, size, at, block)
                dq = jnp.zeros((block, LANES), jnp.float32)
                dk = jnp.zeros((size, LANES), jnp.float32)
                dv = jnp.zeros((size, LANES), jnp.float32)
                for head in range(2):
                    own_query = query * masks[head]
                    own_grad = grad * masks[head]
                    scores = jnp.where(same, dot_nt(keys, own_query), -1e30)
                    lse = lse_ref[0, pl.ds(head, 1), pl.ds(at, block)]
                    probs = jnp.exp(scores - lse)
                    grad_probs = dot_nt(values, own_grad)
                    inner = jnp.sum(probs * grad_probs, axis=0, keepdims=True)
                    grad_raw = (probs * (grad_probs - inner)).astype(jnp.bfloat16)
                    dv = dv + jnp.dot(
                        probs.astype(jnp.bfloat16), own_grad, preferred_element_type=jnp.float32
                    )
                    dk = dk + jnp.dot(grad_raw, own_query, preferred_element_type=jnp.float32)
                    dq = dq + dot_tn(grad_raw, keys * masks[head])
                dq_acc[pl.ds(at, block), :] = dq
                dk_acc[pl.ds(start, size), :] += dk
                dv_acc[pl.ds(start, size), :] += dv

        return carry

    lax.fori_loop(0, blocks, one_block, 0)
    lane = lax.broadcasted_iota(jnp.int32, (seq, LANES), 1)
    cosine, sine = (cos_ref[...], sin_ref[...])
    dq = dq_acc[...] * (HEAD_DIM**-0.5)
    dk = dk_acc[...]
    dv = dv_acc[...]
    gq = dq * cosine - partner(dq, lane) * sine
    gk = dk * cosine - partner(dk, lane) * sine
    gq_ref[...] = gq.astype(jnp.bfloat16)
    gk_ref[...] = gk.astype(jnp.bfloat16)
    gv_ref[...] = dv.astype(jnp.bfloat16)
    bias_ref[0, 0:1, :] = jnp.sum(gq, axis=0, keepdims=True)
    bias_ref[0, 1:2, :] = jnp.sum(gk, axis=0, keepdims=True)
    bias_ref[0, 2:3, :] = jnp.sum(dv, axis=0, keepdims=True)


def attention_tables(segments):
    rows, seq = segments.shape
    cosine, sine = rotary_tables(positions_of(segments), HEAD_DIM)
    reach = (rows * seq, HEAD_DIM // 2)
    cosine, sine = (cosine.reshape(reach), sine.reshape(reach))
    cos_wide = jnp.concatenate([cosine] * 4, axis=1)
    sin_wide = jnp.concatenate([-sine, sine] * 2, axis=1)
    col = jnp.broadcast_to(segments.reshape(rows * seq, 1), (rows * seq, LANES))
    row = segments.reshape(rows, 1, seq)
    return (cos_wide, sin_wide, col, row)


def attend_forward(qkv, tables, bounds, block):
    cos_wide, sin_wide, col, row = tables
    rows, _, seq = row.shape
    width = qkv.shape[1] // 3
    pairs = width // LANES
    tile = lambda shift: pl.BlockSpec((seq, LANES), lambda r, h, *_: (r, h + shift))
    whole = pl.BlockSpec((seq, LANES), lambda r, h, *_: (r, 0))
    lines = pl.BlockSpec((1, 1, seq), lambda r, h, *_: (r, 0, 0))
    low = jax.ShapeDtypeStruct((rows * seq, width), jnp.bfloat16)
    return pl.pallas_call(
        functools.partial(forward_kernel, block=block),
        grid_spec=pltpu.PrefetchScalarGridSpec(
            num_scalar_prefetch=2,
            grid=(rows, pairs),
            in_specs=[tile(0), tile(pairs), tile(2 * pairs), whole, whole, whole, lines],
            out_specs=[
                tile(0), tile(0), tile(0), tile(0),
                pl.BlockSpec((1, 2, seq), lambda r, h, *_: (r * pairs + h, 0, 0)),
            ],
        ),
        out_shape=[low, low, low, low, jax.ShapeDtypeStruct((rows * pairs, 2, seq), jnp.float32)],
        name="attend_forward",
    )(*bounds, qkv, qkv, qkv, cos_wide, sin_wide, col, row)


def attend_backward(query, key, value, grad_mixed, lse, tables, bounds, block):
    cos_wide, sin_wide, col, row = tables
    rows, _, seq = row.shape
    width = query.shape[1]
    pairs = width // LANES
    tile = pl.BlockSpec((seq, LANES), lambda r, h, *_: (r, h))
    whole = pl.BlockSpec((seq, LANES), lambda r, h, *_: (r, 0))
    lines = pl.BlockSpec((1, 1, seq), lambda r, h, *_: (r, 0, 0))
    low = jax.ShapeDtypeStruct((rows * seq, width), jnp.bfloat16)
    acc = pltpu.VMEM((seq, LANES), jnp.float32)
    return pl.pallas_call(
        functools.partial(backward_kernel, block=block),
        grid_spec=pltpu.PrefetchScalarGridSpec(
            num_scalar_prefetch=2,
            grid=(rows, pairs),
            in_specs=[
                tile, tile, tile, tile,
                pl.BlockSpec((1, 2, seq), lambda r, h, *_: (r * pairs + h, 0, 0)),
                whole, whole, whole, lines,
            ],
            out_specs=[
                tile, tile, tile,
                pl.BlockSpec((1, 3, LANES), lambda r, h, *_: (r, 0, h)),
            ],
            scratch_shapes=[acc, acc, acc],
        ),
        out_shape=[low, low, low, jax.ShapeDtypeStruct((rows, 3, width), jnp.float32)],
        name="attend_backward",
    )(*bounds, query, key, value, grad_mixed, lse, cos_wide, sin_wide, col, row)


def norm_mod(values, gain, bias, shift):
    center = jnp.mean(values, axis=-1, keepdims=True)
    centered = values - center
    spread = jnp.mean(centered * centered, axis=-1, keepdims=True)
    return (centered * lax.rsqrt(spread + 1e-05) * gain + bias) * (1.0 + shift)


def gelu_pair(values):
    cdf = 0.5 * (1.0 + lax.erf(values * (1.0 / math.sqrt(2.0))))
    density = jnp.exp(-0.5 * values * values) * (1.0 / math.sqrt(2.0 * math.pi))
    return (values * cdf, cdf + values * density)


def after(value, *others):
    return lax.optimization_barrier((value, *others))[0]


def product(left, right):
    return jnp.dot(left, right, preferred_element_type=jnp.float32)


def product_left(left, right):
    return lax.dot_general(
        left, right, (((0,), (0,)), ((), ())), preferred_element_type=jnp.float32
    )


def product_right(left, right):
    return lax.dot_general(
        left, right, (((1,), (1,)), ((), ())), preferred_element_type=jnp.float32
    )


def gather(part):
    return lax.all_gather(part, "fsdp", axis=0, tiled=True)


def pack(parts, rows):
    flat = jnp.concatenate(parts, axis=-1)
    room = rows * LANES * -(-flat.shape[-1] // (rows * LANES))
    flat = jnp.pad(flat, ((0, 0), (0, room - flat.shape[-1])))
    return flat.reshape(flat.shape[0] * rows, room // rows)


def unpack(packed, sizes, shards):
    flat = packed.reshape(shards, -1)
    parts, at = ([], 0)
    for size in sizes:
        parts.append(flat[:, at : at + size].reshape(-1))
        at += size
    return parts


def reduce_weight(partial):
    share = lax.psum_scatter(partial, "fsdp", scatter_dimension=0, tiled=True)
    if lax.axis_size("dp") == 2:
        other = lax.ppermute(share, "dp", [(0, 1), (1, 0)])
        return share.astype(jnp.float32) + other.astype(jnp.float32)
    return lax.psum(share.astype(jnp.float32), "dp")


def per_device(
    tokens,
    time_embed,
    segments,
    cotangent,
    attn_norm_gain,
    attn_norm_bias,
    time_weight,
    qkv_weight,
    qkv_bias,
    out_weight,
    out_bias,
    mlp_norm_gain,
    mlp_norm_bias,
    up_weight,
    up_bias,
    down_weight,
    down_bias,
):
    width = tokens.shape[1]
    _, seq = segments.shape
    shards = lax.axis_size("fsdp")
    total_tokens = tokens.shape[0] * lax.axis_size("dp") * shards
    factor = 1.0 / math.sqrt(total_tokens)
    block = min(BLOCK, seq)
    time_rows, time_cols = time_weight.shape

    small = (
        attn_norm_gain, attn_norm_bias, qkv_bias, out_bias,
        mlp_norm_gain, mlp_norm_bias, up_bias, down_bias,
    )
    sizes = [part.shape[0] for part in small]
    fold = qkv_weight.shape[0] // time_rows
    packed = pack([p[None] for p in small], fold * time_rows).reshape(time_rows, -1)
    first = jnp.concatenate([time_weight, packed], axis=1)
    first_cols = first.shape[1]
    one = gather(jnp.concatenate([qkv_weight, first.reshape(fold * time_rows, -1)], axis=1))
    w_qkv = one[:, : qkv_weight.shape[1]]
    first = one[:, qkv_weight.shape[1] :].reshape(shards * time_rows, first_cols)
    two = gather(jnp.concatenate([out_weight, up_weight], axis=1))
    w_out = two[:, :width]
    w_up = two[:, width:]
    w_down = gather(down_weight)
    w_time = first[:, :time_cols]
    gain_one, bias_one, b_qkv, b_out, gain_two, bias_two, b_up, b_down = (
        part.astype(jnp.float32) for part in unpack(first[:, time_cols:], sizes, shards)
    )

    tables = attention_tables(segments)
    bounds = block_bounds(segments, block)
    modulation = product(time_embed, w_time)
    tokens_float = tokens.astype(jnp.float32)
    norm_one, pull_one = jax.vjp(
        norm_mod, tokens_float, gain_one, bias_one, modulation[:, :width]
    )
    normed_one = norm_one.astype(jnp.bfloat16)
    qkv = product(normed_one, w_qkv) + b_qkv
    mixed, query, key, value, lse = attend_forward(qkv, tables, bounds, block)
    hidden = tokens_float + product(mixed, w_out) + b_out
    norm_two, pull_two = jax.vjp(norm_mod, hidden, gain_two, bias_two, modulation[:, width:])
    normed_two = norm_two.astype(jnp.bfloat16)
    up = product(normed_two, w_up) + b_up
    active_float, slope = gelu_pair(up)
    active, slope = lax.optimization_barrier((active_float.astype(jnp.bfloat16), slope))
    grad_out = cotangent.astype(jnp.float32)
    down_sum = product_left(active, cotangent).astype(jnp.bfloat16)
    down_share = reduce_weight(down_sum)
    w_down = after(w_down, down_sum)
    output = hidden + product(active, w_down) + b_down
    layer_out = output.astype(jnp.bfloat16)

    down_bias_sum = jnp.sum(grad_out, axis=0)
    grad_active = product_right(cotangent, w_down)
    grad_up = grad_active * slope
    up_bias_sum = jnp.sum(grad_up, axis=0)
    grad_up_low = grad_up.astype(jnp.bfloat16)
    up_sum = product_left(normed_two, grad_up_low).astype(jnp.bfloat16)
    grad_normed_two = product_right(after(grad_up_low, up_sum), w_up)
    grad_hidden_part, gain_two_sum, bias_two_sum, grad_shift_two = pull_two(grad_normed_two)
    grad_hidden = grad_out + grad_hidden_part
    out_bias_sum = jnp.sum(grad_hidden, axis=0)
    grad_hidden_low = grad_hidden.astype(jnp.bfloat16)
    out_sum = product_left(mixed, grad_hidden_low).astype(jnp.bfloat16)
    two_sum = jnp.concatenate([out_sum, up_sum], axis=1)
    two_share = reduce_weight(two_sum)
    out_share = two_share[:, :width]
    up_share = two_share[:, width:]
    grad_mixed = product_right(after(grad_hidden_low, two_sum), w_out).astype(jnp.bfloat16)
    grad_query, grad_key, grad_value, qkv_bias_rows = attend_backward(
        query, key, value, grad_mixed, lse, tables, bounds, block
    )
    qkv_bias_sum = jnp.sum(qkv_bias_rows, axis=0).reshape(-1)
    grad_qkv_low = jnp.concatenate([grad_query, grad_key, grad_value], axis=1)
    qkv_sum = product_left(normed_one, grad_qkv_low).astype(jnp.bfloat16)
    grad_normed_one = product_right(grad_qkv_low, w_qkv)
    grad_tokens_part, gain_one_sum, bias_one_sum, grad_shift_one = pull_one(grad_normed_one)
    tokens_grad = (grad_hidden + grad_tokens_part).astype(jnp.bfloat16)
    grad_shift = jnp.concatenate([grad_shift_one, grad_shift_two], axis=1).astype(jnp.bfloat16)
    time_sum = product_left(time_embed, grad_shift)
    small_sums = (
        gain_one_sum, bias_one_sum, qkv_bias_sum, out_bias_sum,
        gain_two_sum, bias_two_sum, up_bias_sum, down_bias_sum,
    )
    packed = pack([part.reshape(shards, -1) for part in small_sums], fold * time_rows)
    packed = packed.reshape(shards * time_rows, -1)
    last_sum = jnp.concatenate([time_sum, packed], axis=1).astype(jnp.bfloat16)
    last_sum = last_sum.reshape(qkv_sum.shape[0], -1)
    one_share = reduce_weight(jnp.concatenate([qkv_sum, last_sum], axis=1))
    qkv_share = one_share[:, : qkv_sum.shape[1]]
    last_share = one_share[:, qkv_sum.shape[1] :].reshape(time_rows, first_cols)
    smalls = unpack(last_share[:, time_cols:] * factor, sizes, 1)
    return (
        layer_out,
        tokens_grad,
        smalls[0],
        smalls[1],
        last_share[:, :time_cols] * factor,
        qkv_share * factor,
        smalls[2],
        out_share * factor,
        smalls[3],
        smalls[4],
        smalls[5],
        up_share * factor,
        smalls[6],
        down_share * factor,
        smalls[7],
    )


def solution(mesh):
    placed = (
        P(("dp", "fsdp"), None),
        P(("dp", "fsdp"), None),
        P(("dp", "fsdp"), None),
        P(("dp", "fsdp"), None),
        P("fsdp"),
        P("fsdp"),
        P("fsdp", None),
        P("fsdp", None),
        P("fsdp"),
        P("fsdp", None),
        P("fsdp"),
        P("fsdp"),
        P("fsdp"),
        P("fsdp", None),
        P("fsdp"),
        P("fsdp", None),
        P("fsdp"),
    )

    return jax.shard_map(
        per_device,
        mesh=mesh,
        in_specs=placed,
        out_specs=(
            P(("dp", "fsdp"), None),
            P(("dp", "fsdp"), None),
            P("fsdp"),
            P("fsdp"),
            P("fsdp", None),
            P("fsdp", None),
            P("fsdp"),
            P("fsdp", None),
            P("fsdp"),
            P("fsdp"),
            P("fsdp"),
            P("fsdp", None),
            P("fsdp"),
            P("fsdp", None),
            P("fsdp"),
        ),
        check_vma=False,
    )
```

```python
import functools
import math

import jax
import jax.numpy as jnp
from jax import lax
from jax.experimental import pallas as pl
from jax.experimental.pallas import tpu as pltpu
from jax.sharding import PartitionSpec as P


HEAD_DIM = 64
LANES = 128
BLOCK = 256


def positions_of(segments):
    index = jnp.broadcast_to(jnp.arange(segments.shape[1], dtype=jnp.int32), segments.shape)
    starts = jnp.concatenate(
        [jnp.ones((segments.shape[0], 1), dtype=bool), segments[:, 1:] != segments[:, :-1]], axis=1
    )
    first = lax.cummax(jnp.where(starts, index, jnp.zeros_like(index)), axis=1)
    return index - first


def rotary_tables(positions, head_width):
    steps_half = jnp.arange(head_width // 2, dtype=jnp.float32)
    inverse = jnp.exp(steps_half * (-2.0 * math.log(10000.0) / head_width))
    angles = positions.astype(jnp.float32)[..., None] * inverse
    return (jnp.cos(angles), jnp.sin(angles))


def block_bounds(segments, block):
    rows, seq = segments.shape
    parts = segments.reshape(rows, seq // block, block)
    first, last = (parts[:, :, 0], parts[:, :, -1])
    low = jnp.sum((last[:, None, :] < first[:, :, None]).astype(jnp.int32), axis=-1)
    high = jnp.sum((first[:, None, :] <= last[:, :, None]).astype(jnp.int32), axis=-1)
    return (low, high - low)


def partner(values, lane):
    ahead = pltpu.roll(values, LANES - HEAD_DIM // 2, 1)
    behind = pltpu.roll(values, HEAD_DIM // 2, 1)
    return jnp.where(lane % HEAD_DIM < HEAD_DIM // 2, ahead, behind)


def head_masks():
    lane = lax.broadcasted_iota(jnp.int32, (1, LANES), 1)
    own = (lane < HEAD_DIM).astype(jnp.float32)
    return (own.astype(jnp.bfloat16), (1.0 - own).astype(jnp.bfloat16))


def dot_nt(left, right):
    return lax.dot_general(
        left, right, (((1,), (1,)), ((), ())), preferred_element_type=jnp.float32
    )


def dot_tn(left, right):
    return lax.dot_general(
        left, right, (((0,), (0,)), ((), ())), preferred_element_type=jnp.float32
    )


def same_document(col_ref, row_ref, start, size, at, block):
    col = col_ref[pl.ds(start, size), :]
    row = row_ref[0, :, pl.ds(at, block)]
    return jnp.concatenate([col] * (block // LANES), axis=1) == row


def forward_kernel(
    low_ref, count_ref, q_ref, k_ref, v_ref, cos_ref, sin_ref, col_ref, row_ref,
    mixed_ref, query_ref, key_ref, value_ref, lse_ref, *, block
):
    row_at = pl.program_id(0)
    seq = q_ref.shape[0]
    blocks = seq // block
    lane = lax.broadcasted_iota(jnp.int32, (seq, LANES), 1)
    cosine, sine = (cos_ref[...], sin_ref[...])
    q, k = (q_ref[...], k_ref[...])
    rotated = q * cosine + partner(q, lane) * sine
    query_ref[...] = rotated.astype(jnp.bfloat16) * jnp.bfloat16(HEAD_DIM**-0.5)
    key_ref[...] = (k * cosine + partner(k, lane) * sine).astype(jnp.bfloat16)
    value_ref[...] = v_ref[...].astype(jnp.bfloat16)
    masks = head_masks()

    def one_block(i, carry):
        at = pl.multiple_of(i * block, block)
        low = low_ref[row_at, i]
        count = count_ref[row_at, i]
        start = pl.multiple_of(low * block, block)
        for size_at in range(1, blocks + 1):

            @pl.when(count == size_at)
            def _(size=size_at * block):
                keys = key_ref[pl.ds(start, size), :]
                values = value_ref[pl.ds(start, size), :]
                query = query_ref[pl.ds(at, block), :]
                same = same_document(col_ref, row_ref, start, size, at, block)
                weights = []
                for head in range(2):
                    scores = jnp.where(same, dot_nt(keys, query * masks[head]), -1e30)
                    peak = jnp.max(scores, axis=0, keepdims=True)
                    expo = jnp.exp(scores - peak)
                    total = jnp.sum(expo, axis=0, keepdims=True)
                    lse_ref[0, pl.ds(head, 1), pl.ds(at, block)] = peak + jnp.log(total)
                    weights.append((expo * (1.0 / total)).astype(jnp.bfloat16))
                mixed = dot_tn(weights[0], values * masks[0]) + dot_tn(
                    weights[1], values * masks[1]
                )
                mixed_ref[pl.ds(at, block), :] = mixed.astype(jnp.bfloat16)

        return carry

    lax.fori_loop(0, blocks, one_block, 0)


def backward_kernel(
    low_ref, count_ref, query_ref, key_ref, value_ref, grad_ref, lse_ref, cos_ref, sin_ref,
    col_ref, row_ref, gq_ref, gk_ref, gv_ref, bias_ref, dq_acc, dk_acc, dv_acc, *, block
):
    row_at = pl.program_id(0)
    seq = query_ref.shape[0]
    blocks = seq // block
    dk_acc[...] = jnp.zeros_like(dk_acc)
    dv_acc[...] = jnp.zeros_like(dv_acc)
    masks = head_masks()

    def one_block(i, carry):
        at = pl.multiple_of(i * block, block)
        low = low_ref[row_at, i]
        count = count_ref[row_at, i]
        start = pl.multiple_of(low * block, block)
        for size_at in range(1, blocks + 1):

            @pl.when(count == size_at)
            def _(size=size_at * block):
                keys = key_ref[pl.ds(start, size), :]
                values = value_ref[pl.ds(start, size), :]
                query = query_ref[pl.ds(at, block), :]
                grad = grad_ref[pl.ds(at, block), :]
                same = same_document(col_ref, row_ref, start, size, at, block)
                dq = jnp.zeros((block, LANES), jnp.float32)
                dk = jnp.zeros((size, LANES), jnp.float32)
                dv = jnp.zeros((size, LANES), jnp.float32)
                for head in range(2):
                    own_query = query * masks[head]
                    own_grad = grad * masks[head]
                    scores = jnp.where(same, dot_nt(keys, own_query), -1e30)
                    lse = lse_ref[0, pl.ds(head, 1), pl.ds(at, block)]
                    probs = jnp.exp(scores - lse)
                    grad_probs = dot_nt(values, own_grad)
                    inner = jnp.sum(probs * grad_probs, axis=0, keepdims=True)
                    grad_raw = (probs * (grad_probs - inner)).astype(jnp.bfloat16)
                    dv = dv + jnp.dot(
                        probs.astype(jnp.bfloat16), own_grad, preferred_element_type=jnp.float32
                    )
                    dk = dk + jnp.dot(grad_raw, own_query, preferred_element_type=jnp.float32)
                    dq = dq + dot_tn(grad_raw, keys * masks[head])
                dq_acc[pl.ds(at, block), :] = dq
                dk_acc[pl.ds(start, size), :] += dk
                dv_acc[pl.ds(start, size), :] += dv

        return carry

    lax.fori_loop(0, blocks, one_block, 0)
    lane = lax.broadcasted_iota(jnp.int32, (seq, LANES), 1)
    cosine, sine = (cos_ref[...], sin_ref[...])
    dq = dq_acc[...] * (HEAD_DIM**-0.5)
    dk = dk_acc[...]
    dv = dv_acc[...]
    gq = dq * cosine - partner(dq, lane) * sine
    gk = dk * cosine - partner(dk, lane) * sine
    gq_ref[...] = gq.astype(jnp.bfloat16)
    gk_ref[...] = gk.astype(jnp.bfloat16)
    gv_ref[...] = dv.astype(jnp.bfloat16)
    bias_ref[0, 0:1, :] = jnp.sum(gq, axis=0, keepdims=True)
    bias_ref[0, 1:2, :] = jnp.sum(gk, axis=0, keepdims=True)
    bias_ref[0, 2:3, :] = jnp.sum(dv, axis=0, keepdims=True)


def attention_tables(segments):
    rows, seq = segments.shape
    cosine, sine = rotary_tables(positions_of(segments), HEAD_DIM)
    reach = (rows * seq, HEAD_DIM // 2)
    cosine, sine = (cosine.reshape(reach), sine.reshape(reach))
    cos_wide = jnp.concatenate([cosine] * 4, axis=1)
    sin_wide = jnp.concatenate([-sine, sine] * 2, axis=1)
    col = jnp.broadcast_to(segments.reshape(rows * seq, 1), (rows * seq, LANES))
    row = segments.reshape(rows, 1, seq)
    return (cos_wide, sin_wide, col, row)


def attend_forward(qkv, tables, bounds, block):
    cos_wide, sin_wide, col, row = tables
    rows, _, seq = row.shape
    width = qkv.shape[1] // 3
    pairs = width // LANES
    tile = lambda shift: pl.BlockSpec((seq, LANES), lambda r, h, *_: (r, h + shift))
    whole = pl.BlockSpec((seq, LANES), lambda r, h, *_: (r, 0))
    lines = pl.BlockSpec((1, 1, seq), lambda r, h, *_: (r, 0, 0))
    low = jax.ShapeDtypeStruct((rows * seq, width), jnp.bfloat16)
    return pl.pallas_call(
        functools.partial(forward_kernel, block=block),
        grid_spec=pltpu.PrefetchScalarGridSpec(
            num_scalar_prefetch=2,
            grid=(rows, pairs),
            in_specs=[tile(0), tile(pairs), tile(2 * pairs), whole, whole, whole, lines],
            out_specs=[
                tile(0), tile(0), tile(0), tile(0),
                pl.BlockSpec((1, 2, seq), lambda r, h, *_: (r * pairs + h, 0, 0)),
            ],
        ),
        out_shape=[low, low, low, low, jax.ShapeDtypeStruct((rows * pairs, 2, seq), jnp.float32)],
        name="attend_forward",
    )(*bounds, qkv, qkv, qkv, cos_wide, sin_wide, col, row)


def attend_backward(query, key, value, grad_mixed, lse, tables, bounds, block):
    cos_wide, sin_wide, col, row = tables
    rows, _, seq = row.shape
    width = query.shape[1]
    pairs = width // LANES
    tile = pl.BlockSpec((seq, LANES), lambda r, h, *_: (r, h))
    whole = pl.BlockSpec((seq, LANES), lambda r, h, *_: (r, 0))
    lines = pl.BlockSpec((1, 1, seq), lambda r, h, *_: (r, 0, 0))
    low = jax.ShapeDtypeStruct((rows * seq, width), jnp.bfloat16)
    acc = pltpu.VMEM((seq, LANES), jnp.float32)
    return pl.pallas_call(
        functools.partial(backward_kernel, block=block),
        grid_spec=pltpu.PrefetchScalarGridSpec(
            num_scalar_prefetch=2,
            grid=(rows, pairs),
            in_specs=[
                tile, tile, tile, tile,
                pl.BlockSpec((1, 2, seq), lambda r, h, *_: (r * pairs + h, 0, 0)),
                whole, whole, whole, lines,
            ],
            out_specs=[
                tile, tile, tile,
                pl.BlockSpec((1, 3, LANES), lambda r, h, *_: (r, 0, h)),
            ],
            scratch_shapes=[acc, acc, acc],
        ),
        out_shape=[low, low, low, jax.ShapeDtypeStruct((rows, 3, width), jnp.float32)],
        name="attend_backward",
    )(*bounds, query, key, value, grad_mixed, lse, cos_wide, sin_wide, col, row)


def norm_mod(values, gain, bias, shift):
    center = jnp.mean(values, axis=-1, keepdims=True)
    centered = values - center
    spread = jnp.mean(centered * centered, axis=-1, keepdims=True)
    return (centered * lax.rsqrt(spread + 1e-05) * gain + bias) * (1.0 + shift)


def gelu_pair(values):
    cdf = 0.5 * (1.0 + lax.erf(values * (1.0 / math.sqrt(2.0))))
    density = jnp.exp(-0.5 * values * values) * (1.0 / math.sqrt(2.0 * math.pi))
    return (values * cdf, cdf + values * density)


def after(value, *others):
    return lax.optimization_barrier((value, *others))[0]


def product(left, right):
    return jnp.dot(left, right, preferred_element_type=jnp.float32)


def product_left(left, right):
    return lax.dot_general(
        left, right, (((0,), (0,)), ((), ())), preferred_element_type=jnp.float32
    )


def product_right(left, right):
    return lax.dot_general(
        left, right, (((1,), (1,)), ((), ())), preferred_element_type=jnp.float32
    )


def gather(part):
    return lax.all_gather(part, "fsdp", axis=0, tiled=True)


def pack(parts, rows):
    flat = jnp.concatenate(parts, axis=-1)
    room = rows * LANES * -(-flat.shape[-1] // (rows * LANES))
    flat = jnp.pad(flat, ((0, 0), (0, room - flat.shape[-1])))
    return flat.reshape(flat.shape[0] * rows, room // rows)


def unpack(packed, sizes, shards):
    flat = packed.reshape(shards, -1)
    parts, at = ([], 0)
    for size in sizes:
        parts.append(flat[:, at : at + size].reshape(-1))
        at += size
    return parts


def plane_share(partial):
    if lax.axis_size("dp") != 2:
        return partial
    rows, cols = (partial.shape[0] // 2, partial.shape[1] // 2)
    plane, core = (lax.axis_index("dp"), lax.axis_index("fsdp") % 2)

    def part(core_at, plane_at):
        return lax.dynamic_slice(partial, (core_at * rows, plane_at * cols), (rows, cols))

    shards = lax.axis_size("fsdp")
    sent = lax.ppermute(
        part(1 - core, 1 - plane), "fsdp", [(i, i ^ 1) for i in range(shards)]
    )
    both = part(core, 1 - plane).astype(jnp.float32) + sent.astype(jnp.float32)
    other = lax.ppermute(both.astype(jnp.bfloat16), "dp", [(0, 1), (1, 0)])
    kept = part(core, plane).astype(jnp.float32) + other.astype(jnp.float32)
    mine = lax.dynamic_slice(partial, (0, plane * cols), (2 * rows, cols))
    return lax.dynamic_update_slice(mine, kept.astype(jnp.bfloat16), (core * rows, 0))


def reduce_planes(shares):
    share = lax.psum_scatter(
        jnp.concatenate(shares, axis=1), "fsdp", scatter_dimension=0, tiled=True
    )
    cuts = [sum(s.shape[1] for s in shares[:i]) for i in range(1, len(shares))]
    if lax.axis_size("dp") != 2:
        total = lax.psum(share.astype(jnp.float32), "dp")
        return jnp.split(total, cuts, axis=1)
    other = lax.ppermute(share, "dp", [(0, 1), (1, 0)])
    first = lax.axis_index("dp") == 0
    left = jnp.where(first, share, other).astype(jnp.float32)
    right = jnp.where(first, other, share).astype(jnp.float32)
    return [
        jnp.concatenate(pair, axis=1)
        for pair in zip(jnp.split(left, cuts, axis=1), jnp.split(right, cuts, axis=1))
    ]


def reduce_weight(partial):
    share = lax.psum_scatter(partial, "fsdp", scatter_dimension=0, tiled=True)
    if lax.axis_size("dp") == 2:
        other = lax.ppermute(share, "dp", [(0, 1), (1, 0)])
        return share.astype(jnp.float32) + other.astype(jnp.float32)
    return lax.psum(share.astype(jnp.float32), "dp")


def per_device(
    tokens,
    time_embed,
    segments,
    cotangent,
    attn_norm_gain,
    attn_norm_bias,
    time_weight,
    qkv_weight,
    qkv_bias,
    out_weight,
    out_bias,
    mlp_norm_gain,
    mlp_norm_bias,
    up_weight,
    up_bias,
    down_weight,
    down_bias,
):
    width = tokens.shape[1]
    _, seq = segments.shape
    shards = lax.axis_size("fsdp")
    total_tokens = tokens.shape[0] * lax.axis_size("dp") * shards
    factor = 1.0 / math.sqrt(total_tokens)
    block = min(BLOCK, seq)
    time_rows, time_cols = time_weight.shape

    small = (
        attn_norm_gain, attn_norm_bias, qkv_bias, out_bias,
        mlp_norm_gain, mlp_norm_bias, up_bias, down_bias,
    )
    sizes = [part.shape[0] for part in small]
    fold = qkv_weight.shape[0] // time_rows
    packed = pack([p[None] for p in small], fold * time_rows).reshape(time_rows, -1)
    first = jnp.concatenate([time_weight, packed], axis=1)
    first_cols = first.shape[1]
    one = gather(jnp.concatenate([qkv_weight, first.reshape(fold * time_rows, -1)], axis=1))
    w_qkv = one[:, : qkv_weight.shape[1]]
    first = one[:, qkv_weight.shape[1] :].reshape(shards * time_rows, first_cols)
    two = gather(jnp.concatenate([out_weight, up_weight], axis=1))
    w_out = two[:, :width]
    w_up = two[:, width:]
    w_down = gather(down_weight)
    w_time = first[:, :time_cols]
    gain_one, bias_one, b_qkv, b_out, gain_two, bias_two, b_up, b_down = (
        part.astype(jnp.float32) for part in unpack(first[:, time_cols:], sizes, shards)
    )

    tables = attention_tables(segments)
    bounds = block_bounds(segments, block)
    modulation = product(time_embed, w_time)
    tokens_float = tokens.astype(jnp.float32)
    norm_one, pull_one = jax.vjp(
        norm_mod, tokens_float, gain_one, bias_one, modulation[:, :width]
    )
    normed_one = norm_one.astype(jnp.bfloat16)
    qkv = product(normed_one, w_qkv) + b_qkv
    mixed, query, key, value, lse = attend_forward(qkv, tables, bounds, block)
    hidden = tokens_float + product(mixed, w_out) + b_out
    norm_two, pull_two = jax.vjp(norm_mod, hidden, gain_two, bias_two, modulation[:, width:])
    normed_two = norm_two.astype(jnp.bfloat16)
    up = product(normed_two, w_up) + b_up
    active_float, slope = gelu_pair(up)
    active, slope = lax.optimization_barrier((active_float.astype(jnp.bfloat16), slope))
    grad_out = cotangent.astype(jnp.float32)
    down_sum = product_left(active, cotangent).astype(jnp.bfloat16)
    down_share = reduce_weight(down_sum)
    w_down = after(w_down, down_sum)
    output = hidden + product(active, w_down) + b_down
    layer_out = output.astype(jnp.bfloat16)

    down_bias_sum = jnp.sum(grad_out, axis=0)
    grad_active = product_right(cotangent, w_down)
    grad_up = grad_active * slope
    up_bias_sum = jnp.sum(grad_up, axis=0)
    grad_up_low = grad_up.astype(jnp.bfloat16)
    up_sum = product_left(normed_two, grad_up_low).astype(jnp.bfloat16)
    up_half = plane_share(up_sum)
    grad_normed_two = product_right(after(grad_up_low, up_sum), w_up)
    grad_hidden_part, gain_two_sum, bias_two_sum, grad_shift_two = pull_two(grad_normed_two)
    grad_hidden = grad_out + grad_hidden_part
    out_bias_sum = jnp.sum(grad_hidden, axis=0)
    grad_hidden_low = grad_hidden.astype(jnp.bfloat16)
    out_sum = product_left(mixed, grad_hidden_low).astype(jnp.bfloat16)
    out_half = plane_share(out_sum)
    out_share, up_share = reduce_planes([out_half, up_half])
    grad_mixed = product_right(after(grad_hidden_low, out_sum), w_out).astype(jnp.bfloat16)
    grad_query, grad_key, grad_value, qkv_bias_rows = attend_backward(
        query, key, value, grad_mixed, lse, tables, bounds, block
    )
    qkv_bias_sum = jnp.sum(qkv_bias_rows, axis=0).reshape(-1)
    grad_qkv_low = jnp.concatenate([grad_query, grad_key, grad_value], axis=1)
    qkv_sum = product_left(normed_one, grad_qkv_low).astype(jnp.bfloat16)
    qkv_half = plane_share(qkv_sum)
    grad_normed_one = product_right(after(grad_qkv_low, qkv_sum), w_qkv)
    grad_tokens_part, gain_one_sum, bias_one_sum, grad_shift_one = pull_one(grad_normed_one)
    tokens_grad = (grad_hidden + grad_tokens_part).astype(jnp.bfloat16)
    grad_shift = jnp.concatenate([grad_shift_one, grad_shift_two], axis=1).astype(jnp.bfloat16)
    time_sum = product_left(time_embed, grad_shift)
    small_sums = (
        gain_one_sum, bias_one_sum, qkv_bias_sum, out_bias_sum,
        gain_two_sum, bias_two_sum, up_bias_sum, down_bias_sum,
    )
    packed = pack([part.reshape(shards, -1) for part in small_sums], fold * time_rows)
    packed = packed.reshape(shards * time_rows, -1)
    last_sum = jnp.concatenate([time_sum, packed], axis=1).astype(jnp.bfloat16)
    last_sum = last_sum.reshape(qkv_sum.shape[0], -1)
    last_cols = last_sum.shape[1]
    last_sum = jnp.pad(last_sum, ((0, 0), (0, -last_cols % (2 * LANES))))
    last_half = plane_share(last_sum)
    qkv_share, last_share = reduce_planes([qkv_half, last_half])
    last_share = last_share[:, :last_cols].reshape(time_rows, first_cols)
    smalls = unpack(last_share[:, time_cols:] * factor, sizes, 1)
    return (
        layer_out,
        tokens_grad,
        smalls[0],
        smalls[1],
        last_share[:, :time_cols] * factor,
        qkv_share * factor,
        smalls[2],
        out_share * factor,
        smalls[3],
        smalls[4],
        smalls[5],
        up_share * factor,
        smalls[6],
        down_share * factor,
        smalls[7],
    )


def solution(mesh):
    placed = (
        P(("dp", "fsdp"), None),
        P(("dp", "fsdp"), None),
        P(("dp", "fsdp"), None),
        P(("dp", "fsdp"), None),
        P("fsdp"),
        P("fsdp"),
        P("fsdp", None),
        P("fsdp", None),
        P("fsdp"),
        P("fsdp", None),
        P("fsdp"),
        P("fsdp"),
        P("fsdp"),
        P("fsdp", None),
        P("fsdp"),
        P("fsdp", None),
        P("fsdp"),
    )

    return jax.shard_map(
        per_device,
        mesh=mesh,
        in_specs=placed,
        out_specs=(
            P(("dp", "fsdp"), None),
            P(("dp", "fsdp"), None),
            P("fsdp"),
            P("fsdp"),
            P("fsdp", None),
            P("fsdp", None),
            P("fsdp"),
            P("fsdp", None),
            P("fsdp"),
            P("fsdp"),
            P("fsdp"),
            P("fsdp", None),
            P("fsdp"),
            P("fsdp", None),
            P("fsdp"),
        ),
        check_vma=False,
    )
```

```python
import functools
import math

import jax
import jax.numpy as jnp
from jax import lax
from jax.experimental import pallas as pl
from jax.experimental.pallas import tpu as pltpu
from jax.sharding import PartitionSpec as P


HEAD_DIM = 64
LANES = 128
BLOCK = 256


def positions_of(segments):
    index = jnp.broadcast_to(jnp.arange(segments.shape[1], dtype=jnp.int32), segments.shape)
    starts = jnp.concatenate(
        [jnp.ones((segments.shape[0], 1), dtype=bool), segments[:, 1:] != segments[:, :-1]], axis=1
    )
    first = lax.cummax(jnp.where(starts, index, jnp.zeros_like(index)), axis=1)
    return index - first


def rotary_tables(positions, head_width):
    steps_half = jnp.arange(head_width // 2, dtype=jnp.float32)
    inverse = jnp.exp(steps_half * (-2.0 * math.log(10000.0) / head_width))
    angles = positions.astype(jnp.float32)[..., None] * inverse
    return (jnp.cos(angles), jnp.sin(angles))


def block_bounds(segments, block):
    rows, seq = segments.shape
    parts = segments.reshape(rows, seq // block, block)
    first, last = (parts[:, :, 0], parts[:, :, -1])
    low = jnp.sum((last[:, None, :] < first[:, :, None]).astype(jnp.int32), axis=-1)
    high = jnp.sum((first[:, None, :] <= last[:, :, None]).astype(jnp.int32), axis=-1)
    return (low, high - low)


def partner(values, lane):
    ahead = pltpu.roll(values, LANES - HEAD_DIM // 2, 1)
    behind = pltpu.roll(values, HEAD_DIM // 2, 1)
    return jnp.where(lane % HEAD_DIM < HEAD_DIM // 2, ahead, behind)


def head_masks():
    lane = lax.broadcasted_iota(jnp.int32, (1, LANES), 1)
    own = (lane < HEAD_DIM).astype(jnp.float32)
    return (own.astype(jnp.bfloat16), (1.0 - own).astype(jnp.bfloat16))


def dot_nt(left, right):
    return lax.dot_general(
        left, right, (((1,), (1,)), ((), ())), preferred_element_type=jnp.float32
    )


def dot_tn(left, right):
    return lax.dot_general(
        left, right, (((0,), (0,)), ((), ())), preferred_element_type=jnp.float32
    )


def same_document(col_ref, row_ref, start, size, at, block):
    col = col_ref[pl.ds(start, size), :]
    row = row_ref[0, :, pl.ds(at, block)]
    return jnp.concatenate([col] * (block // LANES), axis=1) == row


def forward_kernel(
    low_ref, count_ref, q_ref, k_ref, v_ref, cos_ref, sin_ref, col_ref, row_ref,
    mixed_ref, query_ref, key_ref, value_ref, lse_ref, *, block
):
    row_at = pl.program_id(0)
    seq = q_ref.shape[0]
    blocks = seq // block
    lane = lax.broadcasted_iota(jnp.int32, (seq, LANES), 1)
    cosine, sine = (cos_ref[...], sin_ref[...])
    q, k = (q_ref[...], k_ref[...])
    rotated = q * cosine + partner(q, lane) * sine
    query_ref[...] = rotated.astype(jnp.bfloat16) * jnp.bfloat16(HEAD_DIM**-0.5)
    key_ref[...] = (k * cosine + partner(k, lane) * sine).astype(jnp.bfloat16)
    value_ref[...] = v_ref[...].astype(jnp.bfloat16)
    masks = head_masks()

    def one_block(i, carry):
        at = pl.multiple_of(i * block, block)
        low = low_ref[row_at, i]
        count = count_ref[row_at, i]
        start = pl.multiple_of(low * block, block)
        for size_at in range(1, blocks + 1):

            @pl.when(count == size_at)
            def _(size=size_at * block):
                keys = key_ref[pl.ds(start, size), :]
                values = value_ref[pl.ds(start, size), :]
                query = query_ref[pl.ds(at, block), :]
                same = same_document(col_ref, row_ref, start, size, at, block)
                weights = []
                for head in range(2):
                    scores = jnp.where(same, dot_nt(keys, query * masks[head]), -1e30)
                    peak = jnp.max(scores, axis=0, keepdims=True)
                    expo = jnp.exp(scores - peak)
                    total = jnp.sum(expo, axis=0, keepdims=True)
                    lse_ref[0, pl.ds(head, 1), pl.ds(at, block)] = peak + jnp.log(total)
                    weights.append((expo * (1.0 / total)).astype(jnp.bfloat16))
                mixed = dot_tn(weights[0], values * masks[0]) + dot_tn(
                    weights[1], values * masks[1]
                )
                mixed_ref[pl.ds(at, block), :] = mixed.astype(jnp.bfloat16)

        return carry

    lax.fori_loop(0, blocks, one_block, 0)


def backward_kernel(
    low_ref, count_ref, query_ref, key_ref, value_ref, grad_ref, lse_ref, cos_ref, sin_ref,
    col_ref, row_ref, gq_ref, gk_ref, gv_ref, bias_ref, dq_acc, dk_acc, dv_acc, *, block
):
    row_at = pl.program_id(0)
    seq = query_ref.shape[0]
    blocks = seq // block
    dk_acc[...] = jnp.zeros_like(dk_acc)
    dv_acc[...] = jnp.zeros_like(dv_acc)
    masks = head_masks()

    def one_block(i, carry):
        at = pl.multiple_of(i * block, block)
        low = low_ref[row_at, i]
        count = count_ref[row_at, i]
        start = pl.multiple_of(low * block, block)
        for size_at in range(1, blocks + 1):

            @pl.when(count == size_at)
            def _(size=size_at * block):
                keys = key_ref[pl.ds(start, size), :]
                values = value_ref[pl.ds(start, size), :]
                query = query_ref[pl.ds(at, block), :]
                grad = grad_ref[pl.ds(at, block), :]
                same = same_document(col_ref, row_ref, start, size, at, block)
                dq = jnp.zeros((block, LANES), jnp.float32)
                dk = jnp.zeros((size, LANES), jnp.float32)
                dv = jnp.zeros((size, LANES), jnp.float32)
                for head in range(2):
                    own_query = query * masks[head]
                    own_grad = grad * masks[head]
                    scores = jnp.where(same, dot_nt(keys, own_query), -1e30)
                    lse = lse_ref[0, pl.ds(head, 1), pl.ds(at, block)]
                    probs = jnp.exp(scores - lse)
                    grad_probs = dot_nt(values, own_grad)
                    inner = jnp.sum(probs * grad_probs, axis=0, keepdims=True)
                    grad_raw = (probs * (grad_probs - inner)).astype(jnp.bfloat16)
                    dv = dv + jnp.dot(
                        probs.astype(jnp.bfloat16), own_grad, preferred_element_type=jnp.float32
                    )
                    dk = dk + jnp.dot(grad_raw, own_query, preferred_element_type=jnp.float32)
                    dq = dq + dot_tn(grad_raw, keys * masks[head])
                dq_acc[pl.ds(at, block), :] = dq
                dk_acc[pl.ds(start, size), :] += dk
                dv_acc[pl.ds(start, size), :] += dv

        return carry

    lax.fori_loop(0, blocks, one_block, 0)
    lane = lax.broadcasted_iota(jnp.int32, (seq, LANES), 1)
    cosine, sine = (cos_ref[...], sin_ref[...])
    dq = dq_acc[...] * (HEAD_DIM**-0.5)
    dk = dk_acc[...]
    dv = dv_acc[...]
    gq = dq * cosine - partner(dq, lane) * sine
    gk = dk * cosine - partner(dk, lane) * sine
    gq_ref[...] = gq.astype(jnp.bfloat16)
    gk_ref[...] = gk.astype(jnp.bfloat16)
    gv_ref[...] = dv.astype(jnp.bfloat16)
    bias_ref[0, 0:1, :] = jnp.sum(gq, axis=0, keepdims=True)
    bias_ref[0, 1:2, :] = jnp.sum(gk, axis=0, keepdims=True)
    bias_ref[0, 2:3, :] = jnp.sum(dv, axis=0, keepdims=True)


def attention_tables(segments):
    rows, seq = segments.shape
    cosine, sine = rotary_tables(positions_of(segments), HEAD_DIM)
    reach = (rows * seq, HEAD_DIM // 2)
    cosine, sine = (cosine.reshape(reach), sine.reshape(reach))
    cos_wide = jnp.concatenate([cosine] * 4, axis=1)
    sin_wide = jnp.concatenate([-sine, sine] * 2, axis=1)
    col = jnp.broadcast_to(segments.reshape(rows * seq, 1), (rows * seq, LANES))
    row = segments.reshape(rows, 1, seq)
    return (cos_wide, sin_wide, col, row)


def attend_forward(qkv, tables, bounds, block):
    cos_wide, sin_wide, col, row = tables
    rows, _, seq = row.shape
    width = qkv.shape[1] // 3
    pairs = width // LANES
    tile = lambda shift: pl.BlockSpec((seq, LANES), lambda r, h, *_: (r, h + shift))
    whole = pl.BlockSpec((seq, LANES), lambda r, h, *_: (r, 0))
    lines = pl.BlockSpec((1, 1, seq), lambda r, h, *_: (r, 0, 0))
    low = jax.ShapeDtypeStruct((rows * seq, width), jnp.bfloat16)
    return pl.pallas_call(
        functools.partial(forward_kernel, block=block),
        grid_spec=pltpu.PrefetchScalarGridSpec(
            num_scalar_prefetch=2,
            grid=(rows, pairs),
            in_specs=[tile(0), tile(pairs), tile(2 * pairs), whole, whole, whole, lines],
            out_specs=[
                tile(0), tile(0), tile(0), tile(0),
                pl.BlockSpec((1, 2, seq), lambda r, h, *_: (r * pairs + h, 0, 0)),
            ],
        ),
        out_shape=[low, low, low, low, jax.ShapeDtypeStruct((rows * pairs, 2, seq), jnp.float32)],
        name="attend_forward",
    )(*bounds, qkv, qkv, qkv, cos_wide, sin_wide, col, row)


def attend_backward(query, key, value, grad_mixed, lse, tables, bounds, block):
    cos_wide, sin_wide, col, row = tables
    rows, _, seq = row.shape
    width = query.shape[1]
    pairs = width // LANES
    tile = pl.BlockSpec((seq, LANES), lambda r, h, *_: (r, h))
    whole = pl.BlockSpec((seq, LANES), lambda r, h, *_: (r, 0))
    lines = pl.BlockSpec((1, 1, seq), lambda r, h, *_: (r, 0, 0))
    low = jax.ShapeDtypeStruct((rows * seq, width), jnp.bfloat16)
    acc = pltpu.VMEM((seq, LANES), jnp.float32)
    return pl.pallas_call(
        functools.partial(backward_kernel, block=block),
        grid_spec=pltpu.PrefetchScalarGridSpec(
            num_scalar_prefetch=2,
            grid=(rows, pairs),
            in_specs=[
                tile, tile, tile, tile,
                pl.BlockSpec((1, 2, seq), lambda r, h, *_: (r * pairs + h, 0, 0)),
                whole, whole, whole, lines,
            ],
            out_specs=[
                tile, tile, tile,
                pl.BlockSpec((1, 3, LANES), lambda r, h, *_: (r, 0, h)),
            ],
            scratch_shapes=[acc, acc, acc],
        ),
        out_shape=[low, low, low, jax.ShapeDtypeStruct((rows, 3, width), jnp.float32)],
        name="attend_backward",
    )(*bounds, query, key, value, grad_mixed, lse, cos_wide, sin_wide, col, row)


def norm_mod(values, gain, bias, shift):
    center = jnp.mean(values, axis=-1, keepdims=True)
    centered = values - center
    spread = jnp.mean(centered * centered, axis=-1, keepdims=True)
    return (centered * lax.rsqrt(spread + 1e-05) * gain + bias) * (1.0 + shift)


def gelu_pair(values):
    cdf = 0.5 * (1.0 + lax.erf(values * (1.0 / math.sqrt(2.0))))
    density = jnp.exp(-0.5 * values * values) * (1.0 / math.sqrt(2.0 * math.pi))
    return (values * cdf, cdf + values * density)


def after(value, *others):
    return lax.optimization_barrier((value, *others))[0]


def product(left, right):
    return jnp.dot(left, right, preferred_element_type=jnp.float32)


def product_left(left, right):
    return lax.dot_general(
        left, right, (((0,), (0,)), ((), ())), preferred_element_type=jnp.float32
    )


def product_right(left, right):
    return lax.dot_general(
        left, right, (((1,), (1,)), ((), ())), preferred_element_type=jnp.float32
    )


def gather(part):
    return lax.all_gather(part, "fsdp", axis=0, tiled=True)


def pack(parts, rows):
    flat = jnp.concatenate(parts, axis=-1)
    room = rows * LANES * -(-flat.shape[-1] // (rows * LANES))
    flat = jnp.pad(flat, ((0, 0), (0, room - flat.shape[-1])))
    return flat.reshape(flat.shape[0] * rows, room // rows)


def unpack(packed, sizes, shards):
    flat = packed.reshape(shards, -1)
    parts, at = ([], 0)
    for size in sizes:
        parts.append(flat[:, at : at + size].reshape(-1))
        at += size
    return parts


def plane_share(partial):
    if lax.axis_size("dp") != 2:
        return (partial, partial)
    rows, cols = (partial.shape[0] // 2, partial.shape[1] // 2)
    plane, core = (lax.axis_index("dp"), lax.axis_index("fsdp") % 2)

    def part(core_at, plane_at):
        return lax.dynamic_slice(partial, (core_at * rows, plane_at * cols), (rows, cols))

    shards = lax.axis_size("fsdp")
    sent = lax.ppermute(
        part(1 - core, 1 - plane), "fsdp", [(i, i ^ 1) for i in range(shards)]
    )
    both = part(core, 1 - plane).astype(jnp.float32) + sent.astype(jnp.float32)
    both = both.astype(jnp.bfloat16)
    other = lax.ppermute(both, "dp", [(0, 1), (1, 0)])
    kept = part(core, plane).astype(jnp.float32) + other.astype(jnp.float32)
    mine = lax.dynamic_slice(partial, (0, plane * cols), (2 * rows, cols))
    return (lax.dynamic_update_slice(mine, kept.astype(jnp.bfloat16), (core * rows, 0)), both)


def reduce_planes(shares):
    share = lax.psum_scatter(
        jnp.concatenate(shares, axis=1), "fsdp", scatter_dimension=0, tiled=True
    )
    cuts = [sum(s.shape[1] for s in shares[:i]) for i in range(1, len(shares))]
    if lax.axis_size("dp") != 2:
        total = lax.psum(share.astype(jnp.float32), "dp")
        return jnp.split(total, cuts, axis=1)
    other = lax.ppermute(share, "dp", [(0, 1), (1, 0)])
    first = lax.axis_index("dp") == 0
    left = jnp.where(first, share, other).astype(jnp.float32)
    right = jnp.where(first, other, share).astype(jnp.float32)
    return [
        jnp.concatenate(pair, axis=1)
        for pair in zip(jnp.split(left, cuts, axis=1), jnp.split(right, cuts, axis=1))
    ]


def reduce_weight(partial):
    share = lax.psum_scatter(partial, "fsdp", scatter_dimension=0, tiled=True)
    if lax.axis_size("dp") == 2:
        other = lax.ppermute(share, "dp", [(0, 1), (1, 0)])
        return share.astype(jnp.float32) + other.astype(jnp.float32)
    return lax.psum(share.astype(jnp.float32), "dp")


def per_device(
    tokens,
    time_embed,
    segments,
    cotangent,
    attn_norm_gain,
    attn_norm_bias,
    time_weight,
    qkv_weight,
    qkv_bias,
    out_weight,
    out_bias,
    mlp_norm_gain,
    mlp_norm_bias,
    up_weight,
    up_bias,
    down_weight,
    down_bias,
):
    width = tokens.shape[1]
    _, seq = segments.shape
    shards = lax.axis_size("fsdp")
    total_tokens = tokens.shape[0] * lax.axis_size("dp") * shards
    factor = 1.0 / math.sqrt(total_tokens)
    block = min(BLOCK, seq)
    time_rows, time_cols = time_weight.shape

    small = (
        attn_norm_gain, attn_norm_bias, qkv_bias, out_bias,
        mlp_norm_gain, mlp_norm_bias, up_bias, down_bias,
    )
    sizes = [part.shape[0] for part in small]
    fold = qkv_weight.shape[0] // time_rows
    packed = pack([p[None] for p in small], fold * time_rows).reshape(time_rows, -1)
    first = jnp.concatenate([time_weight, packed], axis=1)
    first_cols = first.shape[1]
    one = gather(jnp.concatenate([qkv_weight, first.reshape(fold * time_rows, -1)], axis=1))
    w_qkv = one[:, : qkv_weight.shape[1]]
    first = one[:, qkv_weight.shape[1] :].reshape(shards * time_rows, first_cols)
    two = gather(jnp.concatenate([out_weight, up_weight], axis=1))
    w_out = two[:, :width]
    w_up = two[:, width:]
    w_down = gather(down_weight)
    w_time = first[:, :time_cols]
    gain_one, bias_one, b_qkv, b_out, gain_two, bias_two, b_up, b_down = (
        part.astype(jnp.float32) for part in unpack(first[:, time_cols:], sizes, shards)
    )

    tables = attention_tables(segments)
    bounds = block_bounds(segments, block)
    modulation = product(time_embed, w_time)
    tokens_float = tokens.astype(jnp.float32)
    norm_one, pull_one = jax.vjp(
        norm_mod, tokens_float, gain_one, bias_one, modulation[:, :width]
    )
    normed_one = norm_one.astype(jnp.bfloat16)
    qkv = product(normed_one, w_qkv) + b_qkv
    mixed, query, key, value, lse = attend_forward(qkv, tables, bounds, block)
    hidden = tokens_float + product(mixed, w_out) + b_out
    norm_two, pull_two = jax.vjp(norm_mod, hidden, gain_two, bias_two, modulation[:, width:])
    normed_two = norm_two.astype(jnp.bfloat16)
    up = product(normed_two, w_up) + b_up
    active_float, slope = gelu_pair(up)
    active, slope = lax.optimization_barrier((active_float.astype(jnp.bfloat16), slope))
    grad_out = cotangent.astype(jnp.float32)
    down_sum = product_left(active, cotangent).astype(jnp.bfloat16)
    down_share = reduce_weight(down_sum)
    w_down = after(w_down, down_sum)
    output = hidden + product(active, w_down) + b_down
    layer_out = output.astype(jnp.bfloat16)

    down_bias_sum = jnp.sum(grad_out, axis=0)
    grad_active = product_right(cotangent, w_down)
    grad_up = grad_active * slope
    up_bias_sum = jnp.sum(grad_up, axis=0)
    grad_up_low = grad_up.astype(jnp.bfloat16)
    up_sum = product_left(normed_two, grad_up_low).astype(jnp.bfloat16)
    up_half, _ = plane_share(up_sum)
    grad_normed_two = product_right(after(grad_up_low, up_sum), w_up)
    grad_hidden_part, gain_two_sum, bias_two_sum, grad_shift_two = pull_two(grad_normed_two)
    grad_hidden = grad_out + grad_hidden_part
    out_bias_sum = jnp.sum(grad_hidden, axis=0)
    grad_hidden_low = grad_hidden.astype(jnp.bfloat16)
    out_sum = product_left(mixed, grad_hidden_low).astype(jnp.bfloat16)
    out_half, _ = plane_share(out_sum)
    out_share, up_share = reduce_planes([out_half, up_half])
    grad_mixed = product_right(after(grad_hidden_low, out_sum), w_out).astype(jnp.bfloat16)
    grad_query, grad_key, grad_value, qkv_bias_rows = attend_backward(
        query, key, value, grad_mixed, lse, tables, bounds, block
    )
    qkv_bias_sum = jnp.sum(qkv_bias_rows, axis=0).reshape(-1)
    grad_query, grad_key, grad_value, _ = lax.optimization_barrier(
        (grad_query, grad_key, grad_value, up_half)
    )
    grad_qkv_low = jnp.concatenate([grad_query, grad_key, grad_value], axis=1)
    qkv_sum = product_left(normed_one, grad_qkv_low).astype(jnp.bfloat16)
    qkv_half, qkv_sent = plane_share(qkv_sum)
    grad_normed_one = product_right(after(grad_qkv_low, qkv_sent), w_qkv)
    grad_tokens_part, gain_one_sum, bias_one_sum, grad_shift_one = pull_one(grad_normed_one)
    tokens_grad = (grad_hidden + grad_tokens_part).astype(jnp.bfloat16)
    grad_shift = jnp.concatenate([grad_shift_one, grad_shift_two], axis=1).astype(jnp.bfloat16)
    time_sum = product_left(time_embed, grad_shift)
    small_sums = (
        gain_one_sum, bias_one_sum, qkv_bias_sum, out_bias_sum,
        gain_two_sum, bias_two_sum, up_bias_sum, down_bias_sum,
    )
    packed = pack([part.reshape(shards, -1) for part in small_sums], fold * time_rows)
    packed = packed.reshape(shards * time_rows, -1)
    last_sum = jnp.concatenate([time_sum, packed], axis=1).astype(jnp.bfloat16)
    last_sum = last_sum.reshape(qkv_sum.shape[0], -1)
    last_cols = last_sum.shape[1]
    last_sum = jnp.pad(last_sum, ((0, 0), (0, -last_cols % (2 * LANES))))
    last_half, _ = plane_share(last_sum)
    qkv_share, last_share = reduce_planes([qkv_half, last_half])
    last_share = last_share[:, :last_cols].reshape(time_rows, first_cols)
    smalls = unpack(last_share[:, time_cols:] * factor, sizes, 1)
    return (
        layer_out,
        tokens_grad,
        smalls[0],
        smalls[1],
        last_share[:, :time_cols] * factor,
        qkv_share * factor,
        smalls[2],
        out_share * factor,
        smalls[3],
        smalls[4],
        smalls[5],
        up_share * factor,
        smalls[6],
        down_share * factor,
        smalls[7],
    )


def solution(mesh):
    placed = (
        P(("dp", "fsdp"), None),
        P(("dp", "fsdp"), None),
        P(("dp", "fsdp"), None),
        P(("dp", "fsdp"), None),
        P("fsdp"),
        P("fsdp"),
        P("fsdp", None),
        P("fsdp", None),
        P("fsdp"),
        P("fsdp", None),
        P("fsdp"),
        P("fsdp"),
        P("fsdp"),
        P("fsdp", None),
        P("fsdp"),
        P("fsdp", None),
        P("fsdp"),
    )

    return jax.shard_map(
        per_device,
        mesh=mesh,
        in_specs=placed,
        out_specs=(
            P(("dp", "fsdp"), None),
            P(("dp", "fsdp"), None),
            P("fsdp"),
            P("fsdp"),
            P("fsdp", None),
            P("fsdp", None),
            P("fsdp"),
            P("fsdp", None),
            P("fsdp"),
            P("fsdp"),
            P("fsdp"),
            P("fsdp", None),
            P("fsdp"),
            P("fsdp", None),
            P("fsdp"),
        ),
        check_vma=False,
    )
```
